32 devices in a mesh: row: 4 (over y, x), col: 8 (over z, core).
Axes of the slice: x: 2, y: 2, z: 4, core: 2. Of those that a mesh axis runs over, the one named last changes fastest.
Arguments:
- opening_old: float32 [512, 1024], P('row', 'col'), may hold values from 0.5 to 1.5
- pressure_old: float32 [512, 1024], P('row', 'col'), may hold values from -4 to 4
- injection: float32 [512, 1024], P('row', 'col'), may hold values from 0 to 2
- front_flags: int32 [4, 512], P('row', 'col'), may hold values 0 or 1
- self_kernel: float32 [256, 256], replicated, may hold values from -0.375 to 0.375
- source_column: int32 [4, 512, 4], P('row', 'col'), may hold values from 0 to 7, all different within a row; in each aligned block of 64 rows (0 to 63, 64 to 127, ..., all dimensions but the last counted through in order) at most 64 rows name the same one
- source_tile: int32 [4, 512, 4], P('row', 'col'), may hold values from 0 to 63
- source_rank: int32 [4, 512, 4], P('row', 'col'), may hold values from 1 to 16
- left_factor: float32 [4, 512, 4, 16, 256], P('row', 'col'), may hold values from -1.5 to 1.5
- right_factor: float32 [4, 512, 4, 16, 256], P('row', 'col'), may hold values from -0.375 to 0.375
Outputs:
- opening_new: float32 [512, 1024], P('row', 'col')
- pressure_new: float32 [512, 1024], P('row', 'col')
The draws below stay inside these ranges and needn't reach their ends.
Inputs may be any that keep to these rules, and one draw needn't show every extreme that they name: `source_column`: the 4 sources of a target tile lie in 4 different column blocks; among the 64 target tiles of one device no column block is named more than 64 times, and that count is reached.
All inputs are finite; a program needn't handle non-finite values. No bound on the sum of `front_flags` on one device may be relied on, other than what follows from the above.
Results may differ from the reference program's by a relative error of at most 0.000076.
Values sent between devices are 32-bit elements; how exact they have to be, the bound alone decides.
No kernel may reach another device: no remote copies, remote signals or barrier semaphores. Data moves between devices by JAX's collectives and lax.ppermute only.
A program may use at most 64 MiB of HBM per device.

```python
import math
import jax
import jax.numpy as jnp
import numpy as np
from jax import lax

BR = 128
BC = 128
TSIDE = 16
NB = 4
RMAX = 16
PASSES = 3
TS = 256
T_DEV = 64
CAP = 64
NR = 512
NC = 1024
BANDS = 4
TILE_COLS = 512
N_ROW = 4
N_COL = 8


def set_ends(entries, stream_key, low, largest):
    extent = entries.shape
    index_at = [jax.random.randint(jax.random.fold_in(stream_key, axis), (), 0, extent[axis]) for axis in range(len(extent))]
    entries = entries.at[tuple(index_at)].set(low)
    longest = extent.index(max(extent))
    index_at[longest] = (index_at[longest] + 1) % extent[longest]
    return entries.at[tuple(index_at)].set(largest)


def block_levels(key, extent, shards, smallest, largest):
    loudness, own = 1.0, jax.random.fold_in(key, 6)
    for axis_at, shards_of in shards:
        draws = jnp.exp(jax.random.uniform(jax.random.fold_in(own, axis_at), (shards_of,), jnp.float32, smallest / len(shards), largest / len(shards)))
        loudness = loudness * jnp.repeat(draws, extent[axis_at] // shards_of).reshape([-1 if axis == axis_at else 1 for axis in range(len(extent))])
    return loudness


def deal_out(rng, own, number, rows, number_of, top, limit, slope):
    sequence = jax.random.permutation(rng, number_of)
    packed, ordinary = shares(number_of, rows * top, limit, slope, True), shares(number_of, rows * top, limit, slope, False)
    places = jnp.arange(number_of)

    def named(tallies, turn):
        used = int((tallies > 0).sum())
        fixed = max(1, used // 4)
        shifted = fixed + (places - fixed + turn * (used - fixed)) % max(1, number_of - fixed)
        return jnp.zeros((number_of,), jnp.int32).at[sequence[jnp.where(places < fixed, places, shifted)]].set(jnp.asarray(tallies, jnp.int32))

    tallies = jnp.where(number % 4 == 0, named(packed, number // 4), named(ordinary, number - number // 4 - 1))
    mixed = jax.random.permutation(jax.random.fold_in(own, 3), number_of)
    giver, sink = mixed[0:number_of // 2 * 2:2], mixed[1:number_of // 2 * 2:2]
    room = jnp.minimum(tallies[giver] - 1, limit - tallies[sink]) // 2
    room = jnp.where((giver == sequence[0]) | (sink == sequence[0]) | (tallies[sink] == 0), 0, jnp.maximum(room, 0))
    shifted = jax.random.randint(jax.random.fold_in(own, 4), (number_of // 2,), 0, 1 << 20) % (room + 1)
    tallies = tallies.at[giver].add(-shifted).at[sink].add(shifted)
    labels = jnp.searchsorted(jnp.cumsum(tallies), jnp.arange(rows * top), side="right").astype(jnp.int32)
    table = labels.reshape(top, rows).T
    table = table[jax.random.permutation(jax.random.fold_in(own, 1), rows)]
    turn = jax.random.randint(jax.random.fold_in(own, 2), (rows, 1), 0, top)
    return jnp.take_along_axis(table, (jnp.arange(top)[None, :] + turn) % top, axis=1)


def shares(count, total, limit, skew, full):
    portions = [(1 << 20) // math.isqrt(grade ** skew) + 1 for grade in range(1, count + 1)]
    largest = limit if full else min(limit, max(-(-total // count), total * portions[0] // sum(portions)))
    least = 1 if total - largest >= count - 1 else 0
    counts, surplus = [largest] + [least] * (count - 1), total - largest - least * (count - 1)
    while surplus > 0:
        free = [i for i in range(1, count) if counts[i] < largest] or [i for i in range(1, count) if counts[i] < limit]
        mass, left = sum([portions[i] for i in free]), surplus
        for i in free:
            extra = min(limit - counts[i], max(1, left * portions[i] // mass), surplus)
            counts[i] = counts[i] + extra
            surplus = surplus - extra
    return np.array(counts)


def bell_draw(own_key, dims, spread, reach, split=(), held_as=jnp.bfloat16):
    factor_of = block_levels(own_key, dims, split, -0.22, 0.18) if split else 1.0
    drawn = jax.random.normal(own_key, dims, jnp.float32) * spread * factor_of
    return jnp.minimum(jnp.maximum(drawn, -reach), reach).astype(held_as)


def setup_inputs(seed: int = 0) -> dict:
    keys = jax.random.split(jax.random.key(seed), 11)
    opening_old = jnp.clip(0.5 + 1.0 * jax.random.uniform(keys[0], (NR, NC), jnp.float32) ** block_levels(keys[0], (NR, NC), ((0, 4), (1, 8)), -0.2, 0.2), 0.5, 1.5)
    pressure_old = bell_draw(keys[1], (NR, NC), 1.0, 4.0, ((0, 4), (1, 8)), jnp.float32)
    injection = jnp.clip(2.0 * jax.random.uniform(keys[2], (NR, NC), jnp.float32) ** block_levels(keys[2], (NR, NC), ((0, 4), (1, 8)), -0.2, 0.2), 0.0, 2.0)
    front_flags = set_ends((jax.random.randint(keys[3], (BANDS, TILE_COLS), 0, 4) < 3).astype(jnp.int32), jax.random.fold_in(keys[3], 1), 0, 1)
    self_kernel = bell_draw(keys[4], (TS, TS), TS ** -0.5, 0.375, (), jnp.float32)
    source_column_keys = jax.random.split(jax.random.fold_in(keys[5], 1), BANDS * TILE_COLS // T_DEV)
    source_column_turns = jax.random.permutation(jax.random.fold_in(keys[5], 3), BANDS * TILE_COLS // T_DEV)
    source_column = jax.vmap(lambda own, number: deal_out(jax.random.fold_in(keys[5], 2), own, number, T_DEV, N_COL, NB, CAP, 2))(source_column_keys, source_column_turns).reshape((BANDS, TILE_COLS, NB))
    source_tile = set_ends(jax.random.randint(keys[6], (BANDS, TILE_COLS, NB), 0, T_DEV), jax.random.fold_in(keys[6], 1), 0, T_DEV - 1).astype(jnp.int32)
    source_rank = set_ends(jax.random.randint(keys[7], (BANDS, TILE_COLS, NB), 1, RMAX + 1), jax.random.fold_in(keys[7], 1), 1, RMAX).astype(jnp.int32)
    left_factor = bell_draw(keys[8], (BANDS, TILE_COLS, NB, RMAX, TS), RMAX ** -0.5, 1.5, ((0, 4), (1, 8)), jnp.float32)
    right_factor = bell_draw(keys[9], (BANDS, TILE_COLS, NB, RMAX, TS), TS ** -0.5, 0.375, ((0, 4), (1, 8)), jnp.float32)
    return {"opening_old": opening_old, "pressure_old": pressure_old, "injection": injection, "front_flags": front_flags, "self_kernel": self_kernel, "source_column": source_column, "source_tile": source_tile, "source_rank": source_rank, "left_factor": left_factor, "right_factor": right_factor}


step_size = 0.1
highest_mode = lax.Precision.HIGHEST


def picard_pass(wide_open, wide_press, start_open, inject_part):
    row_count = wide_open.shape[0] - 2
    col_count = wide_open.shape[1] - 2
    cubed_open = wide_open * wide_open * wide_open

    def offset(array, shift_row, shift_col):
        return array[1 + shift_row:1 + shift_row + row_count, 1 + shift_col:1 + shift_col + col_count]

    cube_middle = offset(cubed_open, 0, 0)
    press_middle = offset(wide_press, 0, 0)
    accumulated = jnp.zeros_like(cube_middle)
    for shift_row, shift_col in ((1, 0), (-1, 0), (0, 1), (0, -1)):
        conduct = (cube_middle + offset(cubed_open, shift_row, shift_col)) / 24.0
        accumulated = accumulated + conduct * (offset(wide_press, shift_row, shift_col) - press_middle)
    return start_open + step_size * (accumulated + inject_part)


def reference(opening_old, pressure_old, injection, front_flags, self_kernel, source_column, source_tile, source_rank, left_factor, right_factor):
    current = opening_old
    wide_press = jnp.pad(pressure_old, 1)
    for passes_done in range(PASSES):
        current = picard_pass(jnp.pad(current, 1), wide_press, opening_old, injection)
    row_tiles = BR // TSIDE
    col_tiles = BC // TSIDE
    shaped = current.reshape(N_ROW, row_tiles, TSIDE, N_COL, col_tiles, TSIDE).transpose(0, 3, 1, 4, 2, 5)
    tile_rows = shaped.reshape(N_ROW, N_COL * T_DEV, TS) * front_flags[:, :, None].astype(jnp.float32)
    back = tile_rows.reshape(N_ROW, N_COL, row_tiles, col_tiles, TSIDE, TSIDE).transpose(0, 2, 4, 1, 3, 5)
    opening_new = back.reshape(N_ROW * BR, N_COL * BC)
    index = (source_column * T_DEV + source_tile).astype(jnp.int32).reshape(N_ROW, -1)
    sources = jnp.take_along_axis(tile_rows, index[:, :, None], axis=1).reshape(N_ROW, N_COL * T_DEV, NB, TS)
    rank_keep = (jnp.arange(RMAX)[None, None, None, :] < source_rank[:, :, :, None]).astype(jnp.float32)
    coefficients = jnp.einsum("rtkjs,rtks->rtkj", right_factor, sources, precision=highest_mode) * rank_keep
    near_terms = jnp.einsum("rtkjs,rtkj->rts", left_factor, coefficients, precision=highest_mode)
    self_terms = jnp.einsum("su,rtu->rts", self_kernel, tile_rows, precision=highest_mode)
    pressure_tiles = self_terms + near_terms
    laid = pressure_tiles.reshape(N_ROW, N_COL, row_tiles, col_tiles, TSIDE, TSIDE).transpose(0, 2, 4, 1, 3, 5)
    pressure_new = laid.reshape(N_ROW * BR, N_COL * BC)
    return opening_new, pressure_new
```

```python
import functools

import jax
import jax.numpy as jnp
from jax import lax
from jax.experimental import pallas as pl
from jax.experimental.pallas import tpu as pltpu
from jax.sharding import PartitionSpec as P

TSIDE = 16
PASSES = 3
LANES = 128
SUB = 8
step_size = 0.1


def neighbour_pairs(count, first):
    pairs = [(i, i) for i in range(count)]
    for i in range(first, count - 1, 2):
        pairs[i], pairs[i + 1] = (i, i + 1), (i + 1, i)
    return pairs


def iota(shape, axis):
    return lax.broadcasted_iota(jnp.int32, shape, axis)


def edges_kernel(open_ref, press_ref, inject_ref, rows_ref, cols_ref):
    sub = iota((SUB, LANES), 0)
    lane = iota((SUB, LANES), 1)
    rows = open_ref.shape[0]
    for f, ref in enumerate((open_ref, press_ref, inject_ref)):
        rows_ref[f * SUB : (f + 1) * SUB, :] = jnp.where(
            sub < SUB // 2, ref[0:SUB, :], ref[rows - SUB : rows, :]
        )
        packed = jnp.zeros((SUB, LANES), jnp.float32)
        for g in range(rows // SUB):
            moved = pltpu.roll(ref[g * SUB : (g + 1) * SUB, :], (3 + 8 * g) % LANES, 1)
            packed = jnp.where(lane // 8 == g, moved, packed)
        cols_ref[f * SUB : (f + 1) * SUB, :] = packed


def swap_groups(value):
    sub = iota(value.shape, value.ndim - 2)
    group = iota(value.shape, value.ndim - 1) // TSIDE
    row_axis, lane_axis = value.ndim - 2, value.ndim - 1
    for d in (1, 2, 4):
        low_row, low_group = (sub & d) == 0, (group & d) == 0
        up = pltpu.roll(pltpu.roll(value, SUB - d, row_axis), TSIDE * d, lane_axis)
        down = pltpu.roll(pltpu.roll(value, d, row_axis), LANES - TSIDE * d, lane_axis)
        value = jnp.where(
            low_row == low_group, value, jnp.where(low_row, up, down)
        )
    return value


def picard(opening, pressure, inject, inside):
    rows, cols = opening.shape[-2:]
    row_axis, col_axis = opening.ndim - 2, opening.ndim - 1
    shifts = ((row_axis, rows - 1), (row_axis, 1), (col_axis, cols - 1), (col_axis, 1))
    pressure = jnp.where(inside, pressure, 0.0)
    opening = jnp.where(inside, opening, 0.0)
    base = jnp.where(inside, opening + step_size * inject, 0.0)
    slopes = [
        jnp.where(inside, (pltpu.roll(pressure, s, a) - pressure) * (step_size / 24.0), 0.0)
        for a, s in shifts
    ]
    current = opening
    for _ in range(PASSES):
        cubed = current * current * current
        current = base
        for (a, s), slope in zip(shifts, slopes):
            current = current + (cubed + pltpu.roll(cubed, s, a)) * slope
    return current


def stencil_kernel(
    counts,
    flag_ref,
    flags_ref,
    open_ref,
    press_ref,
    inject_ref,
    rows_a_ref,
    rows_b_ref,
    cols_a_ref,
    cols_b_ref,
    out_ref,
):
    n_row, n_col = counts
    rows, cols = open_ref.shape
    wide, tall = cols + LANES, rows + SUB
    me_row, me_col = lax.axis_index("row"), lax.axis_index("col")
    row_even, col_even = me_row % 2 == 0, me_col % 2 == 0
    sub = iota((SUB, LANES), 0)
    lane = iota((SUB, LANES), 1)
    fields, tails = [], []
    for f, ref in enumerate((open_ref, press_ref, inject_ref)):
        part = slice(f * SUB, (f + 1) * SUB)
        below = jnp.where(row_even, rows_a_ref[part, :], rows_b_ref[part, :])
        above = jnp.where(row_even, rows_b_ref[part, :], rows_a_ref[part, :])
        tail = jnp.where(sub < SUB // 2, below, above)
        right = jnp.where(col_even, cols_a_ref[part, :], cols_b_ref[part, :])
        left = jnp.where(col_even, cols_b_ref[part, :], cols_a_ref[part, :])
        packed = jnp.where(lane % 8 < 3, left, right)
        sides = []
        for g in range(rows // SUB):
            moved = pltpu.roll(packed, (LANES - 3 - 8 * g) % LANES, 1)
            sides.append(jnp.where((lane < 3) | (lane >= LANES - 3), moved, 0.0))
        sides.append(jnp.zeros((SUB, LANES), jnp.float32))
        main = jnp.concatenate([ref[...], tail], axis=0)
        fields.append(jnp.concatenate([main, jnp.concatenate(sides, axis=0)], axis=1))
        tails.append(tail)
    row = iota((tall, wide), 0)
    col = iota((tall, wide), 1)
    row = me_row * rows + jnp.where(row < rows + SUB // 2, row, row - tall)
    col = me_col * cols + jnp.where(col < cols + LANES // 2, col, col - wide)
    inside = (row >= 0) & (row < n_row * rows) & (col >= 0) & (col < n_col * cols)
    current = picard(*fields, inside)[:rows, :cols]
    tiles = swap_groups(current.reshape(rows // SUB, SUB, LANES))
    count = flags_ref.shape[1]
    ones = jnp.where(iota((count, count), 0) == iota((count, count), 1), flags_ref[...], 0)
    flags = jnp.sum(ones.astype(jnp.float32), axis=1, keepdims=True)
    for a in range(rows // TSIDE):
        for h in range(2):
            out_ref[a * 8 : a * 8 + 8, h * LANES : (h + 1) * LANES] = (
                tiles[2 * a + h] * flags[a * 8 : a * 8 + 8, :]
            )
    corner = jnp.zeros((SUB, LANES), jnp.float32)
    for f, ref in enumerate((open_ref, press_ref, inject_ref)):
        top = pltpu.roll(jnp.where(sub < 5, ref[0:SUB, :], tails[f]), 3, 0)
        bottom = pltpu.roll(jnp.where(sub >= 3, ref[rows - SUB : rows, :], tails[f]), 5, 0)
        for b, window in enumerate((top, bottom)):
            at = (f * 2 + b) * 10
            corner = jnp.where(
                (lane >= at + 5) & (lane < at + 10), pltpu.roll(window, at + 5, 1), corner
            )
            corner = jnp.where(
                (lane >= 64 + at) & (lane < 69 + at),
                pltpu.roll(window, (64 + at - (LANES - 5)) % LANES, 1),
                corner,
            )
    out_ref[count : count + SUB, 0:LANES] = corner
    side = cols // TSIDE
    marks = jnp.zeros((SUB, LANES), jnp.float32)
    for at, tile in ((0, 0), (10, count - side), (64, side - 1), (74, count - 1)):
        marks = jnp.where(
            (lane >= at) & (lane < at + 10), flag_ref[0, tile].astype(jnp.float32), marks
        )
    out_ref[count : count + SUB, LANES : 2 * LANES] = marks


def split_dot(left, right):
    dims = (((1,), (1,)), ((), ()))

    def dot(a, b):
        return lax.dot_general(a, b, dims, preferred_element_type=jnp.float32)

    left_high = left.astype(jnp.bfloat16)
    left_low = (left - left_high.astype(jnp.float32)).astype(jnp.bfloat16)
    right_high = right.astype(jnp.bfloat16)
    right_low = (right - right_high.astype(jnp.float32)).astype(jnp.bfloat16)
    return dot(left_high, right_high) + (dot(left_high, right_low) + dot(left_low, right_high))


def pressure_kernel(
    counts,
    column_ref,
    tile_ref,
    rank_ref,
    near_ref,
    far_ref,
    self_ref,
    right_ref,
    left_ref,
    open_out,
    press_out,
    band,
    press,
    fixes,
):
    n_row, n_col = counts
    me_row, me_col = lax.axis_index("row"), lax.axis_index("col")
    count = press.shape[0]
    block = count + SUB
    half = near_ref.shape[0]
    rows, cols = open_out.shape
    side = cols // TSIDE
    sub = iota((SUB, LANES), 0)
    lane = iota((SUB, LANES), 1)
    for h in range(2):
        part = slice(h * LANES, (h + 1) * LANES)
        band[h, 0:half, :] = near_ref[:, part]
        band[h, half : 2 * half, :] = far_ref[:, part]

    def place(column):
        step = column ^ me_col
        return ((step >> 1) + (step & 1) * (n_col // 2)) * block

    starts = [place(c) for c in range(n_col)]
    starts = [pl.multiple_of(s, SUB) for s in starts]
    corners = [[band[h, pl.ds(s + count, SUB), :] for h in range(2)] for s in starts]
    outside = ((sub < 3) & (lane < 10) & (me_row == 0)) | (
        (sub >= 5) & (lane >= 10) & (me_row == n_row - 1)
    )
    left_part = (lane % 10) < 5
    for c in range(n_col - 1):
        a, b = corners[c], corners[c + 1]
        window, marks = (jnp.where(left_part, pltpu.roll(x, 64, 1), y) for x, y in zip(a, b))
        fixed = picard(
            window,
            pltpu.roll(window, LANES - 20, 1),
            pltpu.roll(window, LANES - 40, 1),
            jnp.logical_not(outside),
        )
        fixes[c * SUB : (c + 1) * SUB, :] = fixed * marks
    row_lane = iota((1, LANES), 1)
    for c in range(n_col - 1):
        third = fixes[c * SUB + 3 : c * SUB + 4, :]
        fourth = fixes[c * SUB + 4 : c * SUB + 5, :]
        for start, tile, part, long_row, short_row, long_at, short_at, source in (
            (starts[c], side - 1, 0, third, fourth, (14, 16), (31, 32), (3, 4)),
            (starts[c + 1], 0, 0, third, fourth, (0, 2), (16, 17), (5, 5)),
            (starts[c], count - 1, 1, fourth, third, (126, 128), (111, 112), (13, 14)),
            (starts[c + 1], count - side, 1, fourth, third, (112, 114), (96, 97), (15, 15)),
        ):
            spot = (part, pl.ds(start + tile, 1), slice(None))
            value = band[spot]
            value = jnp.where(
                (row_lane >= long_at[0]) & (row_lane < long_at[1]),
                pltpu.roll(long_row, (long_at[0] - source[0]) % LANES, 1),
                value,
            )
            value = jnp.where(
                row_lane == short_at[0],
                pltpu.roll(short_row, (short_at[0] - source[1]) % LANES, 1),
                value,
            )
            band[spot] = value

    links, ranks = right_ref.shape[1], right_ref.shape[2]
    depth = iota((ranks, LANES), 0)

    def target(t, carry):
        total = jnp.zeros((ranks, 2 * LANES), jnp.float32)
        for k in range(links):
            at = place(column_ref[k, t]) + tile_ref[k, t]
            product = sum(
                right_ref[t, k, :, h * LANES : (h + 1) * LANES] * band[h, pl.ds(at, 1), :]
                for h in range(2)
            )
            coefficient = jnp.sum(product, axis=1, keepdims=True)
            coefficient = jnp.where(depth < rank_ref[k, t], coefficient, 0.0)
            total = total + left_ref[t, k] * jnp.concatenate([coefficient, coefficient], axis=1)
        press[pl.ds(t, 1), :] = jnp.sum(total, axis=0, keepdims=True)
        return carry

    lax.fori_loop(0, count, target, 0, unroll=4)
    own = jnp.concatenate([band[0, 0:count, :], band[1, 0:count, :]], axis=1)
    result = press[...] + split_dot(own, self_ref[...])

    def lay_out(tiles):
        parts = [
            tiles[8 * a : 8 * a + 8, h * LANES : (h + 1) * LANES]
            for a in range(rows // TSIDE)
            for h in range(2)
        ]
        return swap_groups(jnp.stack(parts)).reshape(rows, cols)

    open_out[...] = lay_out(own)
    press_out[...] = lay_out(result)


def local(
    opening_old,
    pressure_old,
    injection,
    front_flags,
    self_kernel,
    source_column,
    source_tile,
    source_rank,
    left_factor,
    right_factor,
):
    n_row, n_col = lax.axis_size("row"), lax.axis_size("col")
    counts = (n_row, n_col)
    rows, cols = opening_old.shape
    count = front_flags.shape[1]
    links = source_column.shape[2]
    vmem = pl.BlockSpec(memory_space=pltpu.VMEM)
    smem = pl.BlockSpec(memory_space=pltpu.SMEM)
    f32 = jnp.float32
    edge_rows, edge_cols = pl.pallas_call(
        edges_kernel,
        out_shape=[jax.ShapeDtypeStruct((3 * SUB, LANES), f32)] * 2,
        in_specs=[vmem] * 3,
        out_specs=[vmem] * 2,
    )(opening_old, pressure_old, injection)
    rows_b = lax.ppermute(edge_rows, "row", neighbour_pairs(n_row, 1))
    rows_a = lax.ppermute(edge_rows, "row", neighbour_pairs(n_row, 0))
    cols_b = lax.ppermute(edge_cols, "col", neighbour_pairs(n_col, 1))
    cols_a = lax.ppermute(edge_cols, "col", neighbour_pairs(n_col, 0))
    block = pl.pallas_call(
        functools.partial(stencil_kernel, counts),
        out_shape=jax.ShapeDtypeStruct((count + SUB, 2 * LANES), f32),
        in_specs=[smem] + [vmem] * 8,
        out_specs=vmem,
    )(
        front_flags,
        front_flags,
        opening_old,
        pressure_old,
        injection,
        rows_a,
        rows_b,
        cols_a,
        cols_b,
    )

    def exchange(value, step):
        return lax.ppermute(value, "col", [(i, i ^ step) for i in range(n_col)])

    near = jnp.concatenate([block] + [exchange(block, s) for s in range(2, n_col, 2)], axis=0)
    far = exchange(near, 1)
    opening_new, pressure_new = pl.pallas_call(
        functools.partial(pressure_kernel, counts),
        out_shape=[jax.ShapeDtypeStruct((rows, cols), f32)] * 2,
        in_specs=[smem] * 3 + [vmem] * 5,
        out_specs=[vmem] * 2,
        scratch_shapes=[
            pltpu.VMEM((2, n_col * (count + SUB), LANES), f32),
            pltpu.VMEM((count, 2 * LANES), f32),
            pltpu.VMEM((n_col * SUB, LANES), f32),
        ],
    )(
        source_column[0].T,
        source_tile[0].T,
        source_rank[0].T,
        near,
        far,
        self_kernel,
        right_factor[0],
        left_factor[0],
    )
    return opening_new, pressure_new


def solution(mesh):
    return jax.shard_map(
        local,
        mesh=mesh,
        in_specs=(
            P("row", "col"),
            P("row", "col"),
            P("row", "col"),
            P("row", "col"),
            P(),
            P("row", "col", None),
            P("row", "col", None),
            P("row", "col", None),
            P("row", "col", None, None, None),
            P("row", "col", None, None, None),
        ),
        out_specs=(P("row", "col"), P("row", "col")),
        check_vma=False,
    )
```

```python
import functools

import jax
import jax.numpy as jnp
from jax import lax
from jax.experimental import pallas as pl
from jax.experimental.pallas import tpu as pltpu
from jax.sharding import PartitionSpec as P


TSIDE = 16
PASSES = 3
GROUP = 8
LANES = 128
SUB = 8
step_size = 0.1


def neighbour_pairs(count, first):
    pairs = [(i, i) for i in range(count)]
    for i in range(first, count - 1, 2):
        pairs[i], pairs[i + 1] = (i, i + 1), (i + 1, i)
    return pairs


def iota(shape, axis):
    return lax.broadcasted_iota(jnp.int32, shape, axis)


def edges_kernel(open_ref, press_ref, inject_ref, fields_ref, rows_ref, cols_ref, sems):
    sub = iota((SUB, LANES), 0)
    lane = iota((SUB, LANES), 1)
    rows = open_ref.shape[0]
    copies = [
        pltpu.make_async_copy(ref, fields_ref.at[f], sems.at[f])
        for f, ref in enumerate((open_ref, press_ref, inject_ref))
    ]
    for copy in copies:
        copy.start()
    for f, copy in enumerate(copies):
        copy.wait()
        ref = fields_ref.at[f]
        rows_ref[f * SUB : (f + 1) * SUB, :] = jnp.where(
            sub < SUB // 2, ref[0:SUB, :], ref[rows - SUB : rows, :]
        )
        packed = jnp.zeros((SUB, LANES), jnp.float32)
        for g in range(rows // SUB):
            moved = pltpu.roll(ref[g * SUB : (g + 1) * SUB, :], (3 + 8 * g) % LANES, 1)
            packed = jnp.where(lane // 8 == g, moved, packed)
        cols_ref[f * SUB : (f + 1) * SUB, :] = packed


def swap_groups(value):
    sub = iota(value.shape, value.ndim - 2)
    group = iota(value.shape, value.ndim - 1) // TSIDE
    row_axis, lane_axis = value.ndim - 2, value.ndim - 1
    for d in (1, 2, 4):
        low_row, low_group = (sub & d) == 0, (group & d) == 0
        up = pltpu.roll(pltpu.roll(value, SUB - d, row_axis), TSIDE * d, lane_axis)
        down = pltpu.roll(pltpu.roll(value, d, row_axis), LANES - TSIDE * d, lane_axis)
        value = jnp.where(
            low_row == low_group, value, jnp.where(low_row, up, down)
        )
    return value


def picard(opening, pressure, inject, inside):
    rows, cols = opening.shape[-2:]
    row_axis, col_axis = opening.ndim - 2, opening.ndim - 1
    shifts = ((row_axis, rows - 1), (row_axis, 1), (col_axis, cols - 1), (col_axis, 1))
    pressure = jnp.where(inside, pressure, 0.0)
    opening = jnp.where(inside, opening, 0.0)
    base = jnp.where(inside, opening + step_size * inject, 0.0)
    slopes = [
        jnp.where(inside, (pltpu.roll(pressure, s, a) - pressure) * (step_size / 24.0), 0.0)
        for a, s in shifts
    ]
    current = opening
    for _ in range(PASSES):
        cubed = current * current * current
        current = base
        for (a, s), slope in zip(shifts, slopes):
            current = current + (cubed + pltpu.roll(cubed, s, a)) * slope
    return current


def stencil_kernel(
    counts,
    flag_ref,
    flags_ref,
    fields_ref,
    rows_a_ref,
    rows_b_ref,
    cols_a_ref,
    cols_b_ref,
    column_ref,
    tile_ref,
    out_ref,
    index_ref,
):
    n_row, n_col = counts
    rows, cols = fields_ref.shape[1:]
    old = [fields_ref.at[f] for f in range(3)]
    wide, tall = cols + LANES, rows + SUB
    me_row, me_col = lax.axis_index("row"), lax.axis_index("col")
    row_even, col_even = me_row % 2 == 0, me_col % 2 == 0
    sub = iota((SUB, LANES), 0)
    lane = iota((SUB, LANES), 1)
    fields, tails = [], []
    for f, ref in enumerate(old):
        part = slice(f * SUB, (f + 1) * SUB)
        below = jnp.where(row_even, rows_a_ref[part, :], rows_b_ref[part, :])
        above = jnp.where(row_even, rows_b_ref[part, :], rows_a_ref[part, :])
        tail = jnp.where(sub < SUB // 2, below, above)
        right = jnp.where(col_even, cols_a_ref[part, :], cols_b_ref[part, :])
        left = jnp.where(col_even, cols_b_ref[part, :], cols_a_ref[part, :])
        packed = jnp.where(lane % 8 < 3, left, right)
        sides = []
        for g in range(rows // SUB):
            moved = pltpu.roll(packed, (LANES - 3 - 8 * g) % LANES, 1)
            sides.append(jnp.where((lane < 3) | (lane >= LANES - 3), moved, 0.0))
        sides.append(jnp.zeros((SUB, LANES), jnp.float32))
        main = jnp.concatenate([ref[...], tail], axis=0)
        fields.append(jnp.concatenate([main, jnp.concatenate(sides, axis=0)], axis=1))
        tails.append(tail)
    row = iota((tall, wide), 0)
    col = iota((tall, wide), 1)
    row = me_row * rows + jnp.where(row < rows + SUB // 2, row, row - tall)
    col = me_col * cols + jnp.where(col < cols + LANES // 2, col, col - wide)
    inside = (row >= 0) & (row < n_row * rows) & (col >= 0) & (col < n_col * cols)
    current = picard(*fields, inside)[:rows, :cols]
    tiles = swap_groups(current.reshape(rows // SUB, SUB, LANES))
    count = flags_ref.shape[1]
    ones = jnp.where(iota((count, count), 0) == iota((count, count), 1), flags_ref[...], 0)
    flags = jnp.sum(ones.astype(jnp.float32), axis=1, keepdims=True)
    for a in range(rows // TSIDE):
        for h in range(2):
            at = h * count + a * SUB
            out_ref[at : at + SUB, :] = tiles[2 * a + h] * flags[a * SUB : a * SUB + SUB, :]
    corner = jnp.zeros((SUB, LANES), jnp.float32)
    for f, ref in enumerate(old):
        top = pltpu.roll(jnp.where(sub < 5, ref[0:SUB, :], tails[f]), 3, 0)
        bottom = pltpu.roll(jnp.where(sub >= 3, ref[rows - SUB : rows, :], tails[f]), 5, 0)
        for b, window in enumerate((top, bottom)):
            at = (f * 2 + b) * 10
            corner = jnp.where(
                (lane >= at + 5) & (lane < at + 10), pltpu.roll(window, at + 5, 1), corner
            )
            corner = jnp.where(
                (lane >= 64 + at) & (lane < 69 + at),
                pltpu.roll(window, (64 + at - (LANES - 5)) % LANES, 1),
                corner,
            )
    side = cols // TSIDE
    for at, tile in ((0, 0), (10, count - side), (69, side - 1), (79, count - 1)):
        corner = jnp.where(
            (lane >= at) & (lane < at + 5), flag_ref[0, tile].astype(jnp.float32), corner
        )
    out_ref[2 * count :, :] = corner
    step = column_ref[...] ^ me_col
    index_ref[...] = ((step >> 1) + (step & 1) * (n_col // 2)) * count + tile_ref[...]


def split_dot(left, right):
    dims = (((1,), (1,)), ((), ()))

    def dot(a, b):
        return lax.dot_general(a, b, dims, preferred_element_type=jnp.float32)

    left_high = left.astype(jnp.bfloat16)
    left_low = (left - left_high.astype(jnp.float32)).astype(jnp.bfloat16)
    right_high = right.astype(jnp.bfloat16)
    right_low = (right - right_high.astype(jnp.float32)).astype(jnp.bfloat16)
    return dot(left_high, right_high) + (dot(left_high, right_low) + dot(left_low, right_high))


def pressure_kernel(counts, index_ref, rank_ref, *refs):
    n_row, n_col = counts
    blocks = refs[:n_col]
    self_ref, right_ref, left_ref, open_out, press_out, band, base, press, around, fixes = refs[n_col:]
    me_row, me_col = lax.axis_index("row"), lax.axis_index("col")
    count = press.shape[1]
    rows, cols = open_out.shape
    sub = iota((SUB, LANES), 0)
    lane = iota((SUB, LANES), 1)
    steps = [2 * i for i in range(n_col // 2)] + [2 * i + 1 for i in range(n_col // 2)]
    columns = [me_col ^ step for step in steps]

    for ref, column in zip(blocks, columns):
        around[pl.ds(pl.multiple_of(column * SUB, SUB), SUB), :] = ref[2 * count :, :]
    corners = [around[c * SUB : (c + 1) * SUB, :] for c in range(n_col)]
    outside = ((sub < 3) & (lane < 10) & (me_row == 0)) | (
        (sub >= 5) & (lane >= 10) & (me_row == n_row - 1)
    )
    left_part = (lane % 10) < 5
    for c in range(n_col - 1):
        a, b = corners[c], corners[c + 1]
        window = jnp.where(left_part, pltpu.roll(a, 64, 1), b)
        marks = jnp.where(left_part, pltpu.roll(a, 59, 1), pltpu.roll(b, 5, 1))
        fixed = picard(
            window,
            pltpu.roll(window, LANES - 20, 1),
            pltpu.roll(window, LANES - 40, 1),
            jnp.logical_not(outside),
        )
        fixes[c * SUB : (c + 1) * SUB, :] = fixed * marks

    def patch(value, fixed, when, moves):
        for row, at, to_row, to, wide in moves:
            moved = pltpu.roll(pltpu.roll(fixed, (to_row - row) % SUB, 0), (to - at) % LANES, 1)
            value = jnp.where(
                (sub == to_row) & (lane >= to) & (lane < to + wide) & when, moved, value
            )
        return value

    last = SUB - 1
    for slot, (ref, column) in enumerate(zip(blocks, columns)):
        before = fixes[pl.ds(pl.multiple_of(jnp.maximum(column - 1, 0) * SUB, SUB), SUB), :]
        after = fixes[pl.ds(pl.multiple_of(jnp.minimum(column, n_col - 2) * SUB, SUB), SUB), :]
        first, final = column > 0, column < n_col - 1
        top = patch(ref[0:SUB, :], before, first, ((3, 5, 0, 0, 2), (4, 5, 0, 16, 1)))
        top = patch(top, after, final, ((3, 3, last, 14, 2), (4, 4, last, 31, 1)))
        bottom = ref[2 * count - SUB : 2 * count, :]
        bottom = patch(bottom, before, first, ((4, 15, 0, 112, 2), (3, 15, 0, 96, 1)))
        bottom = patch(bottom, after, final, ((4, 13, last, 126, 2), (3, 14, last, 111, 1)))
        lower = jnp.concatenate([top, ref[SUB:count, :]], axis=0)
        upper = jnp.concatenate([ref[count : 2 * count - SUB, :], bottom], axis=0)
        band[0, slot * count : (slot + 1) * count, :] = lower
        band[1, slot * count : (slot + 1) * count, :] = upper
        if slot == 0:
            own = (lower, upper)

    def lay_out(lower, upper):
        parts = [
            half[SUB * a : SUB * a + SUB, :] for a in range(rows // TSIDE) for half in (lower, upper)
        ]
        return swap_groups(jnp.stack(parts)).reshape(rows, cols)

    open_out[...] = lay_out(*own)
    base[...] = split_dot(jnp.concatenate(own, axis=1), self_ref[...])

    links, ranks = right_ref.shape[1], right_ref.shape[2]
    depth = iota((ranks, LANES), 0)

    def targets(group, carry):
        for i in range(GROUP):
            t = group * GROUP + i
            total = [jnp.zeros((ranks, LANES), jnp.float32)] * 2
            for k in range(links):
                at = index_ref[k, t]
                product = sum(
                    right_ref[t, k, :, h * LANES : (h + 1) * LANES] * band[h, pl.ds(at, 1), :]
                    for h in range(2)
                )
                coefficient = jnp.sum(product, axis=1, keepdims=True)
                coefficient = jnp.where(depth < rank_ref[k, t], coefficient, 0.0)
                total = [
                    total[h] + left_ref[t, k, :, h * LANES : (h + 1) * LANES] * coefficient
                    for h in range(2)
                ]
            for h in range(2):
                press[h, pl.ds(t, 1), :] = jnp.sum(total[h], axis=0, keepdims=True)
        return carry

    lax.fori_loop(0, count // GROUP, targets, 0)
    press_out[...] = lay_out(*(press[h] + base[:, h * LANES : (h + 1) * LANES] for h in range(2)))


def local(
    opening_old,
    pressure_old,
    injection,
    front_flags,
    self_kernel,
    source_column,
    source_tile,
    source_rank,
    left_factor,
    right_factor,
):
    n_row, n_col = lax.axis_size("row"), lax.axis_size("col")
    counts = (n_row, n_col)
    rows, cols = opening_old.shape
    count = front_flags.shape[1]
    links = source_column.shape[2]
    vmem = pl.BlockSpec(memory_space=pltpu.VMEM)
    smem = pl.BlockSpec(memory_space=pltpu.SMEM)
    f32 = jnp.float32

    def held(value):
        return pltpu.with_memory_space_constraint(value, pltpu.VMEM)

    fields, edge_rows, edge_cols = pl.pallas_call(
        edges_kernel,
        out_shape=[pltpu.VMEM((3, rows, cols), f32)] + [pltpu.VMEM((3 * SUB, LANES), f32)] * 2,
        in_specs=[pl.BlockSpec(memory_space=pltpu.HBM)] * 3,
        out_specs=[vmem] * 3,
        scratch_shapes=[pltpu.SemaphoreType.DMA((3,))],
        compiler_params=pltpu.CompilerParams(vmem_limit_bytes=4 << 20),
        cost_estimate=pl.CostEstimate(flops=4_000_000_000, transcendentals=0, bytes_accessed=30_000_000),
    )(*(pltpu.with_memory_space_constraint(x, pltpu.HBM) for x in (opening_old, pressure_old, injection)))
    rows_b = lax.ppermute(edge_rows, "row", neighbour_pairs(n_row, 1))
    rows_a = lax.ppermute(edge_rows, "row", neighbour_pairs(n_row, 0))
    cols_b = lax.ppermute(edge_cols, "col", neighbour_pairs(n_col, 1))
    cols_a = lax.ppermute(edge_cols, "col", neighbour_pairs(n_col, 0))
    block, index = pl.pallas_call(
        functools.partial(stencil_kernel, counts),
        out_shape=[
            pltpu.VMEM((2 * count + SUB, LANES), f32),
            pltpu.VMEM((links, count), jnp.int32),
        ],
        in_specs=[smem] + [vmem] * 8,
        out_specs=[vmem] * 2,
        compiler_params=pltpu.CompilerParams(vmem_limit_bytes=4 << 20),
        cost_estimate=pl.CostEstimate(
            flops=4_000_000_000, transcendentals=0, bytes_accessed=30_000_000
        ),
    )(
        front_flags,
        front_flags,
        held(fields),
        held(rows_a),
        held(rows_b),
        held(cols_a),
        held(cols_b),
        source_column[0].T,
        source_tile[0].T,
    )

    def exchange(value, step):
        return lax.ppermute(value, "col", [(i, i ^ step) for i in range(n_col)])

    near = [block] + [exchange(block, step) for step in range(2, n_col, 2)]
    far = [exchange(value, 1) for value in near]
    opening_new, pressure_new = pl.pallas_call(
        functools.partial(pressure_kernel, counts),
        out_shape=[jax.ShapeDtypeStruct((rows, cols), f32)] * 2,
        in_specs=[smem] * 2 + [vmem] * (n_col + 3),
        out_specs=[vmem] * 2,
        scratch_shapes=[
            pltpu.VMEM((2, n_col * count, LANES), f32),
            pltpu.VMEM((count, 2 * LANES), f32),
            pltpu.VMEM((2, count, LANES), f32),
            pltpu.VMEM((n_col * SUB, LANES), f32),
            pltpu.VMEM((n_col * SUB, LANES), f32),
        ],
        compiler_params=pltpu.CompilerParams(vmem_limit_bytes=8 << 20),
    )(
        index,
        source_rank[0].T,
        *(held(value) for value in near + far),
        self_kernel,
        right_factor[0],
        left_factor[0],
    )
    return opening_new, pressure_new


def solution(mesh):
    return jax.shard_map(
        local,
        mesh=mesh,
        in_specs=(
            P("row", "col"),
            P("row", "col"),
            P("row", "col"),
            P("row", "col"),
            P(),
            P("row", "col", None),
            P("row", "col", None),
            P("row", "col", None),
            P("row", "col", None, None, None),
            P("row", "col", None, None, None),
        ),
        out_specs=(P("row", "col"), P("row", "col")),
        check_vma=False,
    )
```

```python
import functools

import jax
import jax.numpy as jnp
from jax import lax
from jax.experimental import pallas as pl
from jax.experimental.pallas import tpu as pltpu
from jax.sharding import PartitionSpec as P


TSIDE = 16
PASSES = 3
GROUP = 64
LANES = 128
SUB = 8
step_size = 0.1


def neighbour_pairs(count, first):
    pairs = [(i, i) for i in range(count)]
    for i in range(first, count - 1, 2):
        pairs[i], pairs[i + 1] = (i, i + 1), (i + 1, i)
    return pairs


def iota(shape, axis):
    return lax.broadcasted_iota(jnp.int32, shape, axis)


def edges_kernel(open_ref, press_ref, inject_ref, fields_ref, rows_ref, cols_ref, sems):
    sub = iota((SUB, LANES), 0)
    lane = iota((SUB, LANES), 1)
    rows = open_ref.shape[0]
    copies = [
        pltpu.make_async_copy(ref, fields_ref.at[f], sems.at[f])
        for f, ref in enumerate((open_ref, press_ref, inject_ref))
    ]
    for copy in copies:
        copy.start()
    for f, copy in enumerate(copies):
        copy.wait()
        ref = fields_ref.at[f]
        rows_ref[f * SUB : (f + 1) * SUB, :] = jnp.where(
            sub < SUB // 2, ref[0:SUB, :], ref[rows - SUB : rows, :]
        )
        packed = jnp.zeros((SUB, LANES), jnp.float32)
        for g in range(rows // SUB):
            moved = pltpu.roll(ref[g * SUB : (g + 1) * SUB, :], (3 + 8 * g) % LANES, 1)
            packed = jnp.where(lane // 8 == g, moved, packed)
        cols_ref[f * SUB : (f + 1) * SUB, :] = packed


def swap_groups(value):
    sub = iota(value.shape, value.ndim - 2)
    group = iota(value.shape, value.ndim - 1) // TSIDE
    row_axis, lane_axis = value.ndim - 2, value.ndim - 1
    for d in (1, 2, 4):
        low_row, low_group = (sub & d) == 0, (group & d) == 0
        up = pltpu.roll(pltpu.roll(value, SUB - d, row_axis), TSIDE * d, lane_axis)
        down = up
        if d < 4:
            down = pltpu.roll(pltpu.roll(value, d, row_axis), LANES - TSIDE * d, lane_axis)
        value = jnp.where(
            low_row == low_group, value, jnp.where(low_row, up, down)
        )
    return value


def picard(opening, pressure, inject, inside):
    rows, cols = opening.shape[-2:]
    row_axis, col_axis = opening.ndim - 2, opening.ndim - 1
    shifts = ((row_axis, rows - 1), (row_axis, 1), (col_axis, cols - 1), (col_axis, 1))
    pressure = jnp.where(inside, pressure, 0.0)
    opening = jnp.where(inside, opening, 0.0)
    base = jnp.where(inside, opening + step_size * inject, 0.0)
    slopes = [
        jnp.where(inside, (pltpu.roll(pressure, s, a) - pressure) * (step_size / 24.0), 0.0)
        for a, s in shifts
    ]
    current = opening
    for _ in range(PASSES):
        cubed = current * current * current
        current = base
        for (a, s), slope in zip(shifts, slopes):
            current = current + (cubed + pltpu.roll(cubed, s, a)) * slope
    return current


def strip_picard(mains, strips, tail_inside, strip_inside):
    tall = mains[0].shape[0]
    lane = iota((SUB, LANES), 1)
    sub = iota((SUB, LANES), 0)
    groups = tall // SUB - 1

    def clear(main):
        tail = jnp.where(tail_inside, main[tall - SUB :], 0.0)
        return jnp.concatenate([main[: tall - SUB], tail], axis=0)

    def strip_shifts(value):
        ahead, behind = pltpu.roll(value, SUB - 1, 0), pltpu.roll(value, 1, 0)
        return (
            jnp.where(sub == SUB - 1, pltpu.roll(ahead, LANES - 8, 1), ahead),
            jnp.where(sub == 0, pltpu.roll(behind, 8, 1), behind),
            pltpu.roll(value, LANES - 1, 1),
            pltpu.roll(value, 1, 1),
        )

    def main_shifts(value, sides):
        beyond = jnp.where(
            lane % 8 == 1, pltpu.roll(sides[0], LANES - 1, 1), pltpu.roll(sides[1], LANES - 3, 1)
        )
        moved = [pltpu.roll(beyond, (LANES - 1 - 8 * g) % LANES, 1) for g in range(groups)]
        moved = jnp.concatenate(moved + [jnp.zeros((SUB, LANES), jnp.float32)], axis=0)
        at = iota(value.shape, 1)
        return (
            pltpu.roll(value, tall - 1, 0),
            pltpu.roll(value, 1, 0),
            jnp.where(at == LANES - 1, moved, pltpu.roll(value, LANES - 1, 1)),
            jnp.where(at == 0, moved, pltpu.roll(value, 1, 1)),
        )

    def prepare(shifts, opening, pressure, inject, clear):
        base = clear(opening + step_size * inject)
        return base, [clear((other - pressure) * (step_size / 24.0)) for other in shifts]

    def advance(shifts, cubed, base, slopes):
        current = base
        for other, slope in zip(shifts, slopes):
            current = current + (cubed + other) * slope
        return current

    opening, pressure = clear(mains[0]), clear(mains[1])
    clears = [lambda x, ok=ok: jnp.where(ok, x, 0.0) for ok in strip_inside]
    sides = [[clears[i](strip[i]) for i in range(2)] for strip in strips]
    base, slopes = prepare(main_shifts(pressure, sides[1]), opening, pressure, mains[2], clear)
    edges = [
        prepare(strip_shifts(sides[1][i]), sides[0][i], sides[1][i], sides[2][i], clears[i])
        for i in range(2)
    ]
    current, beside = opening, sides[0]
    for done in range(PASSES):
        cubed = current * current * current
        cubes = [value * value * value for value in beside]
        current = advance(main_shifts(cubed, cubes), cubed, base, slopes)
        if done < PASSES - 1:
            beside = [
                advance(strip_shifts(cube), cube, *edge) for cube, edge in zip(cubes, edges)
            ]
    return current


def stencil_kernel(
    counts,
    flags_ref,
    fields_ref,
    edges_ref,
    rows_a_ref,
    rows_b_ref,
    cols_a_ref,
    cols_b_ref,
    column_ref,
    tile_ref,
    out_ref,
    index_ref,
):
    n_row, n_col = counts
    rows, cols = fields_ref.shape[1:]
    old = [fields_ref.at[f] for f in range(3)]
    me_row, me_col = lax.axis_index("row"), lax.axis_index("col")
    row_even, col_even = me_row % 2 == 0, me_col % 2 == 0
    sub = iota((SUB, LANES), 0)
    lane = iota((SUB, LANES), 1)
    mains, tails, strips = [], [], []
    for f, ref in enumerate(old):
        part = slice(f * SUB, (f + 1) * SUB)
        below = jnp.where(row_even, rows_a_ref[part, :], rows_b_ref[part, :])
        above = jnp.where(row_even, rows_b_ref[part, :], rows_a_ref[part, :])
        tail = jnp.where(sub < SUB // 2, below, above)
        right = jnp.where(col_even, cols_a_ref[part, :], cols_b_ref[part, :])
        left = jnp.where(col_even, cols_b_ref[part, :], cols_a_ref[part, :])
        mine = edges_ref[part, :]
        mains.append(jnp.concatenate([ref[...], tail], axis=0))
        tails.append(tail)
        strips.append(
            (jnp.where(lane % 8 < 3, left, mine), jnp.where(lane % 8 < 3, mine, right))
        )
    tail_inside = ((sub >= SUB // 2) | (me_row < n_row - 1)) & ((sub < SUB // 2) | (me_row > 0))
    strip_inside = ((lane % 8 >= 3) | (me_col > 0), (lane % 8 < 3) | (me_col < n_col - 1))
    current = strip_picard(mains, strips, tail_inside, strip_inside)[:rows]
    tiles = swap_groups(current.reshape(rows // SUB, SUB, LANES))
    count = flags_ref.shape[1]
    ones = jnp.where(iota((count, count), 0) == iota((count, count), 1), flags_ref[...], 0)
    flags = jnp.sum(ones.astype(jnp.float32), axis=1, keepdims=True)
    for a in range(rows // TSIDE):
        for h in range(2):
            at = h * count + a * SUB
            out_ref[at : at + SUB, :] = tiles[2 * a + h] * flags[a * SUB : a * SUB + SUB, :]
    corner = jnp.zeros((SUB, LANES), jnp.float32)
    for f, ref in enumerate(old):
        top = pltpu.roll(jnp.where(sub < 5, ref[0:SUB, :], tails[f]), 3, 0)
        bottom = pltpu.roll(jnp.where(sub >= 3, ref[rows - SUB : rows, :], tails[f]), 5, 0)
        for b, window in enumerate((top, bottom)):
            at = (f * 2 + b) * 10
            corner = jnp.where(
                (lane >= at + 5) & (lane < at + 10), pltpu.roll(window, at + 5, 1), corner
            )
            corner = jnp.where(
                (lane >= 64 + at) & (lane < 69 + at),
                pltpu.roll(window, (64 + at - (LANES - 5)) % LANES, 1),
                corner,
            )
    side = cols // TSIDE
    for at, tile in ((0, 0), (10, count - side), (69, side - 1), (79, count - 1)):
        mark = jnp.broadcast_to(flags[tile : tile + 1, :], (SUB, LANES))
        corner = jnp.where((lane >= at) & (lane < at + 5), mark, corner)
    out_ref[2 * count :, :] = corner
    step = column_ref[...] ^ me_col
    index_ref[...] = ((step >> 1) + (step & 1) * (n_col // 2)) * count + tile_ref[...]


def lay_out(lower, upper):
    parts = [
        half[at : at + SUB, :] for at in range(0, lower.shape[0], SUB) for half in (lower, upper)
    ]
    return swap_groups(jnp.stack(parts)).reshape(len(parts) * SUB, LANES)


def split(value):
    high = value.astype(jnp.bfloat16)
    return high, (value - high.astype(jnp.float32)).astype(jnp.bfloat16)


def split_dot(left, right):
    dims = (((1,), (1,)), ((), ()))

    def dot(a, b):
        return lax.dot_general(a, b, dims, preferred_element_type=jnp.float32)

    return dot(left[0], right[0]) + (dot(left[0], right[1]) + dot(left[1], right[0]))


def self_kernel_of(
    block_ref,
    self_ref,
    index_ref,
    rank_ref,
    open_ref,
    base_ref,
    high_ref,
    low_ref,
    keep_ref,
    index_out,
    rank_out,
    sems,
):
    copies = [
        pltpu.make_async_copy(index_ref, index_out, sems.at[0]),
        pltpu.make_async_copy(rank_ref, rank_out, sems.at[1]),
    ]
    for copy in copies:
        copy.start()
    ranks = keep_ref.shape[1]
    for rank in range(ranks + 1):
        keep_ref[rank] = (iota((ranks, LANES), 0) < rank).astype(jnp.float32)
    count = base_ref.shape[0]
    lower, upper = block_ref[0:count, :], block_ref[count : 2 * count, :]
    open_ref[...] = lay_out(lower, upper)
    parts = split(self_ref[...])
    high_ref[...], low_ref[...] = parts
    base_ref[...] = split_dot(split(jnp.concatenate([lower, upper], axis=1)), parts)
    for copy in copies:
        copy.wait()


def pressure_kernel(counts, index_ref, rank_ref, *refs):
    n_row, n_col = counts
    blocks = refs[:n_col]
    open_ref, base_ref, high_ref, low_ref, keep_ref, right_ref, left_ref = refs[n_col : n_col + 7]
    open_out, press_out, band, press, around, fixes = refs[n_col + 7 :]
    me_row, me_col = lax.axis_index("row"), lax.axis_index("col")
    count = press.shape[1]
    rows, _ = open_out.shape
    sub = iota((SUB, LANES), 0)
    lane = iota((SUB, LANES), 1)
    steps = [2 * i for i in range(n_col // 2)] + [2 * i + 1 for i in range(n_col // 2)]
    columns = [me_col ^ step for step in steps]

    for ref, column in zip(blocks, columns):
        around[pl.ds(pl.multiple_of(column * SUB, SUB), SUB), :] = ref[2 * count :, :]
    corners = [around[c * SUB : (c + 1) * SUB, :] for c in range(n_col)]
    outside = ((sub < 3) & (lane < 10) & (me_row == 0)) | (
        (sub >= 5) & (lane >= 10) & (me_row == n_row - 1)
    )
    left_part = (lane % 10) < 5
    for c in range(n_col - 1):
        a, b = corners[c], corners[c + 1]
        window = jnp.where(left_part, pltpu.roll(a, 64, 1), b)
        marks = jnp.where(left_part, pltpu.roll(a, 59, 1), pltpu.roll(b, 5, 1))
        fixed = picard(
            window,
            pltpu.roll(window, LANES - 20, 1),
            pltpu.roll(window, LANES - 40, 1),
            jnp.logical_not(outside),
        )
        fixes[c * SUB : (c + 1) * SUB, :] = fixed * marks

    def patch(value, fixed, when, moves):
        for row, at, to_row, to, wide in moves:
            moved = pltpu.roll(pltpu.roll(fixed, (to_row - row) % SUB, 0), (to - at) % LANES, 1)
            value = jnp.where(
                (sub == to_row) & (lane >= to) & (lane < to + wide) & when, moved, value
            )
        return value

    last = SUB - 1
    for slot, (ref, column) in enumerate(zip(blocks, columns)):
        before = fixes[pl.ds(pl.multiple_of(jnp.maximum(column - 1, 0) * SUB, SUB), SUB), :]
        after = fixes[pl.ds(pl.multiple_of(jnp.minimum(column, n_col - 2) * SUB, SUB), SUB), :]
        first, final = column > 0, column < n_col - 1
        top = patch(ref[0:SUB, :], before, first, ((3, 5, 0, 0, 2), (4, 5, 0, 16, 1)))
        top = patch(top, after, final, ((3, 3, last, 14, 2), (4, 4, last, 31, 1)))
        bottom = ref[2 * count - SUB : 2 * count, :]
        bottom = patch(bottom, before, first, ((4, 15, 0, 112, 2), (3, 15, 0, 96, 1)))
        bottom = patch(bottom, after, final, ((4, 13, last, 126, 2), (3, 14, last, 111, 1)))
        start = slot * count
        band[0, start : start + SUB, :] = top
        band[0, start + SUB : start + count, :] = ref[SUB:count, :]
        band[1, start : start + count - SUB, :] = ref[count : 2 * count - SUB, :]
        band[1, start + count - SUB : start + count, :] = bottom
        if slot == 0:
            ends = swap_groups(jnp.stack([top, bottom]))
            shift = jnp.concatenate([top - ref[0:SUB, :], bottom - ref[2 * count - SUB : 2 * count, :]])
    open_out[0:SUB, :] = ends[0]
    open_out[SUB : rows - SUB, :] = open_ref[SUB : rows - SUB, :]
    open_out[rows - SUB :, :] = ends[1]
    first_rows = iota((2 * SUB, LANES), 0) < SUB
    shift = jnp.concatenate(
        [jnp.where(first_rows, shift, 0.0), jnp.where(first_rows, 0.0, shift)], axis=1
    )
    moved = split_dot(split(shift), (high_ref[...], low_ref[...]))

    links, ranks = right_ref.shape[1], right_ref.shape[2]

    def half(h):
        return slice(h * LANES, (h + 1) * LANES)

    def target(t):
        total = [None, None]
        for k in range(links):
            at = index_ref[k, t]
            product = sum(right_ref[t, k, :, half(h)] * band[h, pl.ds(at, 1), :] for h in range(2))
            coefficient = jnp.sum(product, axis=1, keepdims=True)
            coefficient = coefficient * keep_ref[rank_ref[k, t]]
            for h in range(2):
                term = left_ref[t, k, :, half(h)] * coefficient
                for at in range(0, ranks, SUB):
                    part = term[at : at + SUB, :]
                    total[h] = part if total[h] is None else total[h] + part
        for h in range(2):
            press[h, pl.ds(t, 1), :] = jnp.sum(total[h], axis=0, keepdims=True)

    def targets(group, carry):
        for i in range(GROUP):
            target(group * GROUP + i)
        return carry

    if GROUP == count:
        for t in range(count):
            target(t)
    else:
        lax.fori_loop(0, count // GROUP, targets, 0)
    base = base_ref[...]
    base = jnp.concatenate(
        [base[:SUB] + moved[:SUB], base[SUB : count - SUB], base[count - SUB :] + moved[SUB:]]
    )
    press_out[...] = lay_out(*(press[h] + base[:, half(h)] for h in range(2)))


def local(
    opening_old,
    pressure_old,
    injection,
    front_flags,
    self_kernel,
    source_column,
    source_tile,
    source_rank,
    left_factor,
    right_factor,
):
    n_row, n_col = lax.axis_size("row"), lax.axis_size("col")
    counts = (n_row, n_col)
    rows, cols = opening_old.shape
    count = front_flags.shape[1]
    links = source_column.shape[2]
    vmem = pl.BlockSpec(memory_space=pltpu.VMEM)
    smem = pl.BlockSpec(memory_space=pltpu.SMEM)
    f32 = jnp.float32

    def held(value):
        return pltpu.with_memory_space_constraint(value, pltpu.VMEM)

    fields, edge_rows, edge_cols = pl.pallas_call(
        edges_kernel,
        out_shape=[pltpu.VMEM((3, rows, cols), f32)] + [pltpu.VMEM((3 * SUB, LANES), f32)] * 2,
        in_specs=[pl.BlockSpec(memory_space=pltpu.HBM)] * 3,
        out_specs=[vmem] * 3,
        scratch_shapes=[pltpu.SemaphoreType.DMA((3,))],
        compiler_params=pltpu.CompilerParams(vmem_limit_bytes=4 << 20),
        cost_estimate=pl.CostEstimate(flops=4_000_000_000, transcendentals=0, bytes_accessed=30_000_000),
    )(*(pltpu.with_memory_space_constraint(x, pltpu.HBM) for x in (opening_old, pressure_old, injection)))
    rows_a = lax.ppermute(edge_rows, "row", neighbour_pairs(n_row, 0))
    if n_row == 4:
        rows_b = lax.ppermute(rows_a, "row", [(i, i ^ 2) for i in range(n_row)])
    else:
        rows_b = lax.ppermute(edge_rows, "row", neighbour_pairs(n_row, 1))
    cols_b = lax.ppermute(edge_cols, "col", neighbour_pairs(n_col, 1))
    cols_a = lax.ppermute(edge_cols, "col", neighbour_pairs(n_col, 0))
    block, index = pl.pallas_call(
        functools.partial(stencil_kernel, counts),
        out_shape=[
            pltpu.VMEM((2 * count + SUB, LANES), f32),
            pltpu.VMEM((links, count), jnp.int32),
        ],
        in_specs=[vmem] * 9,
        out_specs=[vmem] * 2,
        compiler_params=pltpu.CompilerParams(vmem_limit_bytes=4 << 20),
        cost_estimate=pl.CostEstimate(
            flops=4_000_000_000, transcendentals=0, bytes_accessed=30_000_000
        ),
    )(
        front_flags,
        held(fields),
        held(edge_cols),
        held(rows_a),
        held(rows_b),
        held(cols_a),
        held(cols_b),
        source_column[0].T,
        source_tile[0].T,
    )

    def exchange(value, step):
        return lax.ppermute(value, "col", [(i, i ^ step) for i in range(n_col)])

    near = [block] + [exchange(block, step) for step in range(2, n_col, 2)]
    far = [exchange(value, 1) for value in near]
    size, ranks = self_kernel.shape, left_factor.shape[3]
    *own, index, rank = pl.pallas_call(
        self_kernel_of,
        out_shape=[
            pltpu.VMEM((rows, cols), f32),
            pltpu.VMEM((count, size[0]), f32),
            pltpu.VMEM(size, jnp.bfloat16),
            pltpu.VMEM(size, jnp.bfloat16),
            pltpu.VMEM((ranks + 1, ranks, LANES), f32),
            pltpu.SMEM((links, count), jnp.int32),
            pltpu.SMEM((links, count), jnp.int32),
        ],
        in_specs=[vmem] * 4,
        out_specs=[vmem] * 5 + [smem] * 2,
        scratch_shapes=[pltpu.SemaphoreType.DMA((2,))],
        compiler_params=pltpu.CompilerParams(vmem_limit_bytes=4 << 20),
    )(held(block), self_kernel, held(index), source_rank[0].T)
    opening_new, pressure_new = pl.pallas_call(
        functools.partial(pressure_kernel, counts),
        out_shape=[jax.ShapeDtypeStruct((rows, cols), f32)] * 2,
        in_specs=[smem] * 2 + [vmem] * (n_col + 7),
        out_specs=[vmem] * 2,
        scratch_shapes=[
            pltpu.VMEM((2, n_col * count, LANES), f32),
            pltpu.VMEM((2, count, LANES), f32),
            pltpu.VMEM((n_col * SUB, LANES), f32),
            pltpu.VMEM((n_col * SUB, LANES), f32),
        ],
        compiler_params=pltpu.CompilerParams(vmem_limit_bytes=8 << 20),
    )(
        pltpu.with_memory_space_constraint(index, pltpu.SMEM),
        pltpu.with_memory_space_constraint(rank, pltpu.SMEM),
        *(held(value) for value in near + far),
        *(held(value) for value in own),
        right_factor[0],
        left_factor[0],
    )
    return opening_new, pressure_new


def solution(mesh):
    return jax.shard_map(
        local,
        mesh=mesh,
        in_specs=(
            P("row", "col"),
            P("row", "col"),
            P("row", "col"),
            P("row", "col"),
            P(),
            P("row", "col", None),
            P("row", "col", None),
            P("row", "col", None),
            P("row", "col", None, None, None),
            P("row", "col", None, None, None),
        ),
        out_specs=(P("row", "col"), P("row", "col")),
        check_vma=False,
    )
```

```python
import functools

import jax
import jax.numpy as jnp
from jax import lax
from jax.experimental import pallas as pl
from jax.experimental.pallas import tpu as pltpu
from jax.sharding import PartitionSpec as P


TSIDE = 16
PASSES = 3
GROUP = 64
LANES = 128
SUB = 8
step_size = 0.1


def neighbour_pairs(count, first):
    pairs = [(i, i) for i in range(count)]
    for i in range(first, count - 1, 2):
        pairs[i], pairs[i + 1] = (i, i + 1), (i + 1, i)
    return pairs


def iota(shape, axis):
    return lax.broadcasted_iota(jnp.int32, shape, axis)


def edges_kernel(open_ref, press_ref, inject_ref, fields_ref, rows_ref, cols_ref, sems):
    sub = iota((SUB, LANES), 0)
    lane = iota((SUB, LANES), 1)
    rows = open_ref.shape[0]
    copies = [
        pltpu.make_async_copy(ref, fields_ref.at[f], sems.at[f])
        for f, ref in enumerate((open_ref, press_ref, inject_ref))
    ]
    for copy in copies:
        copy.start()
    for f, copy in enumerate(copies):
        copy.wait()
        ref = fields_ref.at[f]
        rows_ref[f * SUB : (f + 1) * SUB, :] = jnp.where(
            sub < SUB // 2, ref[0:SUB, :], ref[rows - SUB : rows, :]
        )
        packed = jnp.zeros((SUB, LANES), jnp.float32)
        for g in range(rows // SUB):
            moved = pltpu.roll(ref[g * SUB : (g + 1) * SUB, :], (3 + 8 * g) % LANES, 1)
            packed = jnp.where(lane // 8 == g, moved, packed)
        cols_ref[f * SUB : (f + 1) * SUB, :] = packed


def swap_groups(value):
    sub = iota(value.shape, value.ndim - 2)
    group = iota(value.shape, value.ndim - 1) // TSIDE
    row_axis, lane_axis = value.ndim - 2, value.ndim - 1
    for d in (1, 2, 4):
        low_row, low_group = (sub & d) == 0, (group & d) == 0
        up = pltpu.roll(pltpu.roll(value, SUB - d, row_axis), TSIDE * d, lane_axis)
        down = up
        if d < 4:
            down = pltpu.roll(pltpu.roll(value, d, row_axis), LANES - TSIDE * d, lane_axis)
        value = jnp.where(
            low_row == low_group, value, jnp.where(low_row, up, down)
        )
    return value


def picard(opening, pressure, inject, inside):
    rows, cols = opening.shape[-2:]
    row_axis, col_axis = opening.ndim - 2, opening.ndim - 1
    shifts = ((row_axis, rows - 1), (row_axis, 1), (col_axis, cols - 1), (col_axis, 1))
    pressure = jnp.where(inside, pressure, 0.0)
    opening = jnp.where(inside, opening, 0.0)
    base = jnp.where(inside, opening + step_size * inject, 0.0)
    slopes = [
        jnp.where(inside, (pltpu.roll(pressure, s, a) - pressure) * (step_size / 24.0), 0.0)
        for a, s in shifts
    ]
    current = opening
    for _ in range(PASSES):
        cubed = current * current * current
        terms = [
            (cubed + pltpu.roll(cubed, s, a)) * slope for (a, s), slope in zip(shifts, slopes)
        ]
        current = (base + terms[0]) + (terms[1] + (terms[2] + terms[3]))
    return current


def strip_picard(mains, strips, tail_inside, strip_inside):
    tall = mains[0].shape[0]
    lane = iota((SUB, LANES), 1)
    sub = iota((SUB, LANES), 0)
    groups = tall // SUB - 1

    def clear(main):
        tail = jnp.where(tail_inside, main[tall - SUB :], 0.0)
        return jnp.concatenate([main[: tall - SUB], tail], axis=0)

    def strip_shifts(value):
        ahead, behind = pltpu.roll(value, SUB - 1, 0), pltpu.roll(value, 1, 0)
        return (
            jnp.where(sub == SUB - 1, pltpu.roll(ahead, LANES - 8, 1), ahead),
            jnp.where(sub == 0, pltpu.roll(behind, 8, 1), behind),
            pltpu.roll(value, LANES - 1, 1),
            pltpu.roll(value, 1, 1),
        )

    def main_shifts(value, sides):
        beyond = jnp.where(
            lane % 8 == 1, pltpu.roll(sides[0], LANES - 1, 1), pltpu.roll(sides[1], LANES - 3, 1)
        )
        moved = [pltpu.roll(beyond, (LANES - 1 - 8 * g) % LANES, 1) for g in range(groups)]
        moved = jnp.concatenate(moved + [jnp.zeros((SUB, LANES), jnp.float32)], axis=0)
        at = iota(value.shape, 1)
        return (
            pltpu.roll(value, tall - 1, 0),
            pltpu.roll(value, 1, 0),
            jnp.where(at == LANES - 1, moved, pltpu.roll(value, LANES - 1, 1)),
            jnp.where(at == 0, moved, pltpu.roll(value, 1, 1)),
        )

    def prepare(shifts, opening, pressure, inject, clear):
        base = clear(opening + step_size * inject)
        return base, [clear((other - pressure) * (step_size / 24.0)) for other in shifts]

    def advance(shifts, cubed, base, slopes):
        terms = [(cubed + other) * slope for other, slope in zip(shifts, slopes)]
        return (base + terms[0]) + (terms[1] + (terms[2] + terms[3]))

    opening, pressure = clear(mains[0]), clear(mains[1])
    clears = [lambda x, ok=ok: jnp.where(ok, x, 0.0) for ok in strip_inside]
    sides = [[clears[i](strip[i]) for i in range(2)] for strip in strips]
    base, slopes = prepare(main_shifts(pressure, sides[1]), opening, pressure, mains[2], clear)
    edges = [
        prepare(strip_shifts(sides[1][i]), sides[0][i], sides[1][i], sides[2][i], clears[i])
        for i in range(2)
    ]
    current, beside = opening, sides[0]
    for done in range(PASSES):
        cubed = current * current * current
        cubes = [value * value * value for value in beside]
        current = advance(main_shifts(cubed, cubes), cubed, base, slopes)
        if done < PASSES - 1:
            beside = [
                advance(strip_shifts(cube), cube, *edge) for cube, edge in zip(cubes, edges)
            ]
    return current


def stencil_kernel(
    counts,
    flags_ref,
    fields_ref,
    edges_ref,
    rows_a_ref,
    rows_b_ref,
    cols_a_ref,
    cols_b_ref,
    column_ref,
    tile_ref,
    out_ref,
    index_ref,
):
    n_row, n_col = counts
    rows, cols = fields_ref.shape[1:]
    old = [fields_ref.at[f] for f in range(3)]
    me_row, me_col = lax.axis_index("row"), lax.axis_index("col")
    row_even, col_even = me_row % 2 == 0, me_col % 2 == 0
    sub = iota((SUB, LANES), 0)
    lane = iota((SUB, LANES), 1)
    mains, tails, strips = [], [], []
    for f, ref in enumerate(old):
        part = slice(f * SUB, (f + 1) * SUB)
        below = jnp.where(row_even, rows_a_ref[part, :], rows_b_ref[part, :])
        above = jnp.where(row_even, rows_b_ref[part, :], rows_a_ref[part, :])
        tail = jnp.where(sub < SUB // 2, below, above)
        right = jnp.where(col_even, cols_a_ref[part, :], cols_b_ref[part, :])
        left = jnp.where(col_even, cols_b_ref[part, :], cols_a_ref[part, :])
        mine = edges_ref[part, :]
        mains.append(jnp.concatenate([ref[...], tail], axis=0))
        tails.append(tail)
        strips.append(
            (jnp.where(lane % 8 < 3, left, mine), jnp.where(lane % 8 < 3, mine, right))
        )
    tail_inside = ((sub >= SUB // 2) | (me_row < n_row - 1)) & ((sub < SUB // 2) | (me_row > 0))
    strip_inside = ((lane % 8 >= 3) | (me_col > 0), (lane % 8 < 3) | (me_col < n_col - 1))
    current = strip_picard(mains, strips, tail_inside, strip_inside)[:rows]
    tiles = swap_groups(current.reshape(rows // SUB, SUB, LANES))
    count = flags_ref.shape[1]
    ones = jnp.where(iota((count, count), 0) == iota((count, count), 1), flags_ref[...], 0)
    flags = jnp.sum(ones.astype(jnp.float32), axis=1, keepdims=True)
    for a in range(rows // TSIDE):
        for h in range(2):
            at = h * count + a * SUB
            out_ref[at : at + SUB, :] = tiles[2 * a + h] * flags[a * SUB : a * SUB + SUB, :]
    corner = jnp.zeros((SUB, LANES), jnp.float32)
    for f, ref in enumerate(old):
        top = pltpu.roll(jnp.where(sub < 5, ref[0:SUB, :], tails[f]), 3, 0)
        bottom = pltpu.roll(jnp.where(sub >= 3, ref[rows - SUB : rows, :], tails[f]), 5, 0)
        for b, window in enumerate((top, bottom)):
            at = (f * 2 + b) * 10
            corner = jnp.where(
                (lane >= at + 5) & (lane < at + 10), pltpu.roll(window, at + 5, 1), corner
            )
            corner = jnp.where(
                (lane >= 64 + at) & (lane < 69 + at),
                pltpu.roll(window, (64 + at - (LANES - 5)) % LANES, 1),
                corner,
            )
    side = cols // TSIDE
    for at, tile in ((0, 0), (10, count - side), (69, side - 1), (79, count - 1)):
        mark = jnp.broadcast_to(flags[tile : tile + 1, :], (SUB, LANES))
        corner = jnp.where((lane >= at) & (lane < at + 5), mark, corner)
    out_ref[2 * count :, :] = corner
    step = column_ref[...] ^ me_col
    index_ref[...] = ((step >> 1) + (step & 1) * (n_col // 2)) * count + tile_ref[...]


def lay_out(lower, upper):
    parts = [
        half[at : at + SUB, :] for at in range(0, lower.shape[0], SUB) for half in (lower, upper)
    ]
    return swap_groups(jnp.stack(parts)).reshape(len(parts) * SUB, LANES)


def split(value, parts=2):
    pieces = []
    for _ in range(parts):
        pieces.append(value.astype(jnp.bfloat16))
        value = value - pieces[-1].astype(jnp.float32)
    return pieces


def split_dot(left, right):
    dims = (((1,), (1,)), ((), ()))
    total = None
    for order in reversed(range(len(left))):
        for i in range(order + 1):
            term = lax.dot_general(
                left[i], right[order - i], dims, preferred_element_type=jnp.float32
            )
            total = term if total is None else total + term
    return total


def self_kernel_of(
    block_ref,
    self_ref,
    index_ref,
    rank_ref,
    open_ref,
    base_ref,
    high_ref,
    low_ref,
    keep_ref,
    index_out,
    rank_out,
    sems,
):
    copies = [
        pltpu.make_async_copy(index_ref, index_out, sems.at[0]),
        pltpu.make_async_copy(rank_ref, rank_out, sems.at[1]),
    ]
    for copy in copies:
        copy.start()
    ranks = keep_ref.shape[1]
    for rank in range(ranks + 1):
        keep_ref[rank] = (iota((ranks, LANES), 0) < rank).astype(jnp.float32)
    count = base_ref.shape[0]
    lower, upper = block_ref[0:count, :], block_ref[count : 2 * count, :]
    open_ref[...] = lay_out(lower, upper)
    parts = split(self_ref[...], 3)
    high_ref[...], low_ref[...] = parts[:2]
    base_ref[...] = split_dot(split(jnp.concatenate([lower, upper], axis=1), 3), parts)
    for copy in copies:
        copy.wait()


def pressure_kernel(counts, index_ref, rank_ref, *refs):
    n_row, n_col = counts
    blocks = refs[:n_col]
    open_ref, base_ref, high_ref, low_ref, keep_ref, right_ref, left_ref = refs[n_col : n_col + 7]
    open_out, press_out, band, press, around, fixes = refs[n_col + 7 :]
    me_row, me_col = lax.axis_index("row"), lax.axis_index("col")
    count = press.shape[1]
    rows, _ = open_out.shape
    sub = iota((SUB, LANES), 0)
    lane = iota((SUB, LANES), 1)
    steps = [2 * i for i in range(n_col // 2)] + [2 * i + 1 for i in range(n_col // 2)]
    columns = [me_col ^ step for step in steps]

    for ref, column in zip(blocks, columns):
        around[pl.ds(pl.multiple_of(column * SUB, SUB), SUB), :] = ref[2 * count :, :]
    corners = [around[c * SUB : (c + 1) * SUB, :] for c in range(n_col)]
    outside = ((sub < 3) & (lane < 10) & (me_row == 0)) | (
        (sub >= 5) & (lane >= 10) & (me_row == n_row - 1)
    )
    left_part = (lane % 10) < 5
    for c in range(n_col - 1):
        a, b = corners[c], corners[c + 1]
        window = jnp.where(left_part, pltpu.roll(a, 64, 1), b)
        marks = jnp.where(left_part, pltpu.roll(a, 59, 1), pltpu.roll(b, 5, 1))
        fixed = picard(
            window,
            pltpu.roll(window, LANES - 20, 1),
            pltpu.roll(window, LANES - 40, 1),
            jnp.logical_not(outside),
        )
        fixes[c * SUB : (c + 1) * SUB, :] = fixed * marks

    def patch(value, fixed, when, moves):
        for row, at, to_row, to, wide in moves:
            moved = pltpu.roll(pltpu.roll(fixed, (to_row - row) % SUB, 0), (to - at) % LANES, 1)
            value = jnp.where(
                (sub == to_row) & (lane >= to) & (lane < to + wide) & when, moved, value
            )
        return value

    last = SUB - 1
    for slot, (ref, column) in enumerate(zip(blocks, columns)):
        before = fixes[pl.ds(pl.multiple_of(jnp.maximum(column - 1, 0) * SUB, SUB), SUB), :]
        after = fixes[pl.ds(pl.multiple_of(jnp.minimum(column, n_col - 2) * SUB, SUB), SUB), :]
        first, final = column > 0, column < n_col - 1
        top = patch(ref[0:SUB, :], before, first, ((3, 5, 0, 0, 2), (4, 5, 0, 16, 1)))
        top = patch(top, after, final, ((3, 3, last, 14, 2), (4, 4, last, 31, 1)))
        bottom = ref[2 * count - SUB : 2 * count, :]
        bottom = patch(bottom, before, first, ((4, 15, 0, 112, 2), (3, 15, 0, 96, 1)))
        bottom = patch(bottom, after, final, ((4, 13, last, 126, 2), (3, 14, last, 111, 1)))
        start = slot * count
        band[0, start : start + SUB, :] = top
        band[0, start + SUB : start + count, :] = ref[SUB:count, :]
        band[1, start : start + count - SUB, :] = ref[count : 2 * count - SUB, :]
        band[1, start + count - SUB : start + count, :] = bottom
        if slot == 0:
            ends = swap_groups(jnp.stack([top, bottom]))
            shift = jnp.concatenate([top - ref[0:SUB, :], bottom - ref[2 * count - SUB : 2 * count, :]])
    open_out[0:SUB, :] = ends[0]
    open_out[SUB : rows - SUB, :] = open_ref[SUB : rows - SUB, :]
    open_out[rows - SUB :, :] = ends[1]
    first_rows = iota((2 * SUB, LANES), 0) < SUB
    shift = jnp.concatenate(
        [jnp.where(first_rows, shift, 0.0), jnp.where(first_rows, 0.0, shift)], axis=1
    )
    moved = split_dot(split(shift), (high_ref[...], low_ref[...]))

    links, ranks = right_ref.shape[1], right_ref.shape[2]

    def half(h):
        return slice(h * LANES, (h + 1) * LANES)

    def target(t):
        total = [None, None]
        for k in range(links):
            at = index_ref[k, t]
            product = sum(right_ref[t, k, :, half(h)] * band[h, pl.ds(at, 1), :] for h in range(2))
            coefficient = jnp.sum(product, axis=1, keepdims=True)
            coefficient = coefficient * keep_ref[rank_ref[k, t]]
            for h in range(2):
                term = left_ref[t, k, :, half(h)] * coefficient
                for at in range(0, ranks, SUB):
                    part = term[at : at + SUB, :]
                    total[h] = part if total[h] is None else total[h] + part
        for h in range(2):
            press[h, pl.ds(t, 1), :] = jnp.sum(total[h], axis=0, keepdims=True)

    def targets(group, carry):
        for i in range(GROUP):
            target(group * GROUP + i)
        return carry

    if GROUP == count:
        for t in range(count):
            target(t)
    else:
        lax.fori_loop(0, count // GROUP, targets, 0)
    base = base_ref[...]
    base = jnp.concatenate(
        [base[:SUB] + moved[:SUB], base[SUB : count - SUB], base[count - SUB :] + moved[SUB:]]
    )
    press_out[...] = lay_out(*(press[h] + base[:, half(h)] for h in range(2)))


def local(
    opening_old,
    pressure_old,
    injection,
    front_flags,
    self_kernel,
    source_column,
    source_tile,
    source_rank,
    left_factor,
    right_factor,
):
    n_row, n_col = lax.axis_size("row"), lax.axis_size("col")
    counts = (n_row, n_col)
    rows, cols = opening_old.shape
    count = front_flags.shape[1]
    links = source_column.shape[2]
    vmem = pl.BlockSpec(memory_space=pltpu.VMEM)
    smem = pl.BlockSpec(memory_space=pltpu.SMEM)
    f32 = jnp.float32

    def held(value):
        return pltpu.with_memory_space_constraint(value, pltpu.VMEM)

    fields, edge_rows, edge_cols = pl.pallas_call(
        edges_kernel,
        out_shape=[pltpu.VMEM((3, rows, cols), f32)] + [pltpu.VMEM((3 * SUB, LANES), f32)] * 2,
        in_specs=[pl.BlockSpec(memory_space=pltpu.HBM)] * 3,
        out_specs=[vmem] * 3,
        scratch_shapes=[pltpu.SemaphoreType.DMA((3,))],
        compiler_params=pltpu.CompilerParams(vmem_limit_bytes=4 << 20),
        cost_estimate=pl.CostEstimate(flops=4_000_000_000, transcendentals=0, bytes_accessed=30_000_000),
    )(*(pltpu.with_memory_space_constraint(x, pltpu.HBM) for x in (opening_old, pressure_old, injection)))
    rows_a = lax.ppermute(edge_rows, "row", neighbour_pairs(n_row, 0))
    if n_row == 4:
        rows_b = lax.ppermute(rows_a, "row", [(i, i ^ 2) for i in range(n_row)])
    else:
        rows_b = lax.ppermute(edge_rows, "row", neighbour_pairs(n_row, 1))
    cols_b = lax.ppermute(edge_cols, "col", neighbour_pairs(n_col, 1))
    cols_a = lax.ppermute(edge_cols, "col", neighbour_pairs(n_col, 0))
    block, index = pl.pallas_call(
        functools.partial(stencil_kernel, counts),
        out_shape=[
            pltpu.VMEM((2 * count + SUB, LANES), f32),
            pltpu.VMEM((links, count), jnp.int32),
        ],
        in_specs=[vmem] * 9,
        out_specs=[vmem] * 2,
        compiler_params=pltpu.CompilerParams(vmem_limit_bytes=4 << 20),
        cost_estimate=pl.CostEstimate(
            flops=4_000_000_000, transcendentals=0, bytes_accessed=30_000_000
        ),
    )(
        front_flags,
        held(fields),
        held(edge_cols),
        held(rows_a),
        held(rows_b),
        held(cols_a),
        held(cols_b),
        source_column[0].T,
        source_tile[0].T,
    )

    def exchange(value, step):
        return lax.ppermute(value, "col", [(i, i ^ step) for i in range(n_col)])

    near = [block] + [exchange(block, step) for step in range(2, n_col, 2)]
    far = [exchange(value, 1) for value in near]
    size, ranks = self_kernel.shape, left_factor.shape[3]
    *own, index, rank = pl.pallas_call(
        self_kernel_of,
        out_shape=[
            pltpu.VMEM((rows, cols), f32),
            pltpu.VMEM((count, size[0]), f32),
            pltpu.VMEM(size, jnp.bfloat16),
            pltpu.VMEM(size, jnp.bfloat16),
            pltpu.VMEM((ranks + 1, ranks, LANES), f32),
            pltpu.SMEM((links, count), jnp.int32),
            pltpu.SMEM((links, count), jnp.int32),
        ],
        in_specs=[vmem] * 4,
        out_specs=[vmem] * 5 + [smem] * 2,
        scratch_shapes=[pltpu.SemaphoreType.DMA((2,))],
        compiler_params=pltpu.CompilerParams(vmem_limit_bytes=4 << 20),
    )(held(block), self_kernel, held(index), source_rank[0].T)
    opening_new, pressure_new = pl.pallas_call(
        functools.partial(pressure_kernel, counts),
        out_shape=[jax.ShapeDtypeStruct((rows, cols), f32)] * 2,
        in_specs=[smem] * 2 + [vmem] * (n_col + 7),
        out_specs=[vmem] * 2,
        scratch_shapes=[
            pltpu.VMEM((2, n_col * count, LANES), f32),
            pltpu.VMEM((2, count, LANES), f32),
            pltpu.VMEM((n_col * SUB, LANES), f32),
            pltpu.VMEM((n_col * SUB, LANES), f32),
        ],
        compiler_params=pltpu.CompilerParams(vmem_limit_bytes=8 << 20),
    )(
        pltpu.with_memory_space_constraint(index, pltpu.SMEM),
        pltpu.with_memory_space_constraint(rank, pltpu.SMEM),
        *(held(value) for value in near + far),
        *(held(value) for value in own),
        right_factor[0],
        left_factor[0],
    )
    return opening_new, pressure_new


def solution(mesh):
    return jax.shard_map(
        local,
        mesh=mesh,
        in_specs=(
            P("row", "col"),
            P("row", "col"),
            P("row", "col"),
            P("row", "col"),
            P(),
            P("row", "col", None),
            P("row", "col", None),
            P("row", "col", None),
            P("row", "col", None, None, None),
            P("row", "col", None, None, None),
        ),
        out_specs=(P("row", "col"), P("row", "col")),
        check_vma=False,
    )
```
